256 devices in a mesh: diff: 128 (over z, x, y_hi, core), obj: 2 (over y_lo).
Axes of the slice: x: 4, y: 4 (y_hi: 2, y_lo: 2; y = y_hi * 2 + y_lo), z: 8, core: 2. Of those that a mesh axis runs over, the one named last changes fastest.
Arguments:
- object_field: float32 [2, 32768, 512], P(None, ('diff', 'obj')), may hold values from -6 to 6
- probe_modes: float32 [4, 2, 256, 256], P('obj'), may hold values from -3 to 3
- amplitudes: float32 [256, 256, 256], P('diff')
- offsets: int32 [256, 2], P('diff'), may hold values from 0 to 256, as said below
- counts: int32 [128], replicated, may hold values from 1 to 2, as said below
Outputs:
- object_out: float32 [2, 32768, 512], P(None, ('diff', 'obj'))
- probe_out: float32 [4, 2, 256, 256], P('obj')
The draws below stay inside these ranges and needn't reach their ends.
Inputs may be any that keep to these rules, and one draw needn't show every extreme that they name: Row k of offsets holds the block-local corner of slot k (block k // 2): offsets[k,0] < 256, and offsets[k,0] <= 0 in the last block; offsets[k,1] <= 256. Every slot, used or not, holds such a corner. Block b uses its first counts[b] slots.
All inputs are finite; a program needn't handle non-finite values.
Results may differ from the reference program's by a relative error of at most 0.0003.
Values sent between devices are 32-bit elements; how exact they have to be, the bound alone decides.
No kernel may reach another device: no remote copies, remote signals or barrier semaphores. Data moves between devices by JAX's collectives and lax.ppermute only.
A program may use at most 64 MiB of HBM per device.

```python
import jax
import jax.numpy as jnp
from jax import lax

PATCH = 256
MODES = 4
SLOTS = 2
TILE_ROWS = 128
COLUMNS = 512
ITERS = 1
PASSES = 3
BLOCK_ROWS = 256
OBJ_ROWS = 32768
POSITIONS = 256
N_DIFF = 128
N_OBJ = 2


def draw_offsets(key, part):
    block_rows = TILE_ROWS * N_OBJ
    positions = jnp.arange(POSITIONS, dtype=jnp.int32)
    block_index = positions // SLOTS
    upper_rows = jnp.where(block_index == N_DIFF - 1, block_rows - PATCH + 1, block_rows)
    rows_drawn = jax.random.randint(jax.random.fold_in(key, 11), (POSITIONS,), 0, upper_rows)
    cols_drawn = jax.random.randint(jax.random.fold_in(key, 12), (POSITIONS,), 0, COLUMNS - PATCH + 1)
    rows_drawn = rows_drawn.at[0].set(block_rows - 1)
    cols_drawn = cols_drawn.at[0].set(COLUMNS - PATCH)
    return jnp.stack([rows_drawn, cols_drawn], axis=1).astype(jnp.int32)


def draw_counts(key, part):
    values = jax.random.randint(jax.random.fold_in(key, 21), (N_DIFF,), 1, SLOTS + 1)
    values = values.at[0].set(SLOTS).at[1].set(1)
    return values.astype(jnp.int32)


def draw_amplitudes(key, part):
    block_index = jnp.arange(POSITIONS, dtype=jnp.int32) // SLOTS
    rising = 1.0 + 2.0 * block_index.astype(jnp.float32) / (N_DIFF - 1)
    shape_all = (POSITIONS, PATCH, PATCH)
    subkey = jax.random.fold_in(key, 31)
    base = jax.random.uniform(subkey, shape_all, minval=0.2, maxval=2.0)
    return (base * rising[:, None, None]).astype(jnp.float32)


def shard_levels(stream_key, shape, split, smallest, top_value):
    def one(axis_at, blocks):
        heights = jax.random.uniform(jax.random.fold_in(jax.random.fold_in(stream_key, 6), axis_at), (blocks,), jnp.float32, smallest / len(split), top_value / len(split))
        return jnp.repeat(jnp.exp(heights), shape[axis_at] // blocks).reshape((-1,) + (1,) * (len(shape) - axis_at - 1))

    loudness = one(*split[0])
    for cut in split[1:]:
        loudness = loudness * one(*cut)
    return loudness


def scatter_about(key, dims, width, most, split=(), kind=jnp.bfloat16):
    drawn = jax.random.normal(key, dims, jnp.float32) * width
    if len(split) > 0:
        drawn = shard_levels(key, dims, split, -0.22, 0.18) * drawn
    return jnp.clip(drawn, min=-most, max=most).astype(kind)


def setup_inputs(seed: int = 0) -> dict:
    keys = jax.random.split(jax.random.key(seed), 6)
    object_field = scatter_about(keys[0], (2, OBJ_ROWS, COLUMNS), 1.0, 6.0, ((1, 256),), jnp.float32)
    probe_modes = scatter_about(keys[1], (MODES, 2, PATCH, PATCH), 0.5, 3.0, ((0, 2),), jnp.float32)
    amplitudes = draw_amplitudes(jax.random.fold_in(keys[5], 71), 0)
    offsets = draw_offsets(jax.random.fold_in(keys[5], 71), 0)
    counts = draw_counts(jax.random.fold_in(keys[5], 71), 0)
    return dict(object_field=object_field, probe_modes=probe_modes, amplitudes=amplitudes, offsets=offsets, counts=counts)


EDGE_SCALE = 1.0
DIFFUSION_RATE = 0.2
OBJECT_STEP = 0.25
HIGHEST = lax.Precision.HIGHEST

def dft_tables(length):
    ladder = jnp.arange(length, dtype=jnp.int32)
    product = ladder[:, None] * ladder[None, :] % length
    angle = product.astype(jnp.float32) * (2.0 * jnp.pi / length)
    scaling = 1.0 / jnp.sqrt(jnp.float32(length))
    return (jnp.cos(angle) * scaling, jnp.sin(angle) * scaling)

def apply_left(table, stacked):
    return jnp.einsum('jk,mkl->mjl', table, stacked, precision=HIGHEST)

def apply_right(stacked, table):
    return jnp.einsum('mjk,kl->mjl', stacked, table, precision=HIGHEST)

def to_detector(real_part, imag_part, cosine, sine_table):
    mid_real = apply_left(cosine, real_part) + apply_left(sine_table, imag_part)
    mid_imag = apply_left(cosine, imag_part) - apply_left(sine_table, real_part)
    out_real = apply_right(mid_real, cosine) + apply_right(mid_imag, sine_table)
    out_imag = apply_right(mid_imag, cosine) - apply_right(mid_real, sine_table)
    return (out_real, out_imag)

def to_sample(real_part, imag_part, cosine, sine_table):
    mid_real = apply_left(cosine, real_part) - apply_left(sine_table, imag_part)
    mid_imag = apply_left(cosine, imag_part) + apply_left(sine_table, real_part)
    out_real = apply_right(mid_real, cosine) - apply_right(mid_imag, sine_table)
    out_imag = apply_right(mid_imag, cosine) + apply_right(mid_real, sine_table)
    return (out_real, out_imag)

def detector_waves(patch_field, probe_modes, cosine, sine_table):
    probe_real = probe_modes[:, 0]
    probe_imag = probe_modes[:, 1]
    wave_real = probe_real * patch_field[0] - probe_imag * patch_field[1]
    wave_imag = probe_real * patch_field[1] + probe_imag * patch_field[0]
    far_real, far_imag = to_detector(wave_real, wave_imag, cosine, sine_table)
    return (far_real, far_imag, lax.optimization_barrier(jnp.sum(far_real * far_real + far_imag * far_imag, axis=0)))

def gradients(patch_field, probe_modes, far_real, far_imag, power, amplitude, cosine, sine_table):
    factor = amplitude / jnp.sqrt(power + 1.0) - 1.0
    back_real, back_imag = to_sample(far_real * factor, far_imag * factor, cosine, sine_table)
    probe_real = probe_modes[:, 0]
    probe_imag = probe_modes[:, 1]
    patch_grad = jnp.stack([lax.optimization_barrier(jnp.sum(probe_real * back_real + probe_imag * back_imag, axis=0)), lax.optimization_barrier(jnp.sum(probe_real * back_imag - probe_imag * back_real, axis=0))])
    probe_grad = jnp.stack([patch_field[0] * back_real + patch_field[1] * back_imag, patch_field[0] * back_imag - patch_field[1] * back_real], axis=1)
    return (patch_grad, probe_grad)

def edge_flux(difference):
    weight = 1.0 / (1.0 + lax.optimization_barrier(jnp.sum(difference * difference, axis=0, keepdims=True)) / (EDGE_SCALE * EDGE_SCALE))
    return difference * weight

def diffuse(stacked, row_ids, total_rows):
    center = stacked[:, 1:-1]
    inner_ids = row_ids[1:-1]
    valid_up = ((inner_ids >= 1) & (inner_ids <= total_rows)).astype(stacked.dtype)
    valid_down = ((inner_ids >= -1) & (inner_ids < total_rows - 1)).astype(stacked.dtype)
    upward = edge_flux(stacked[:, :-2] - center) * valid_up[None, :, None]
    downward = edge_flux(stacked[:, 2:] - center) * valid_down[None, :, None]
    across = edge_flux(center[:, :, 1:] - center[:, :, :-1])
    zero_column = jnp.zeros_like(center[:, :, :1])
    sideways = jnp.concatenate([across, zero_column], axis=2) - jnp.concatenate([zero_column, across], axis=2)
    return center + DIFFUSION_RATE * (upward + downward + sideways)

def reference(object_field, probe_modes, amplitudes, offsets, counts):
    cosine, sine_table = dft_tables(PATCH)
    total_rows = BLOCK_ROWS * N_DIFF
    for iteration in range(ITERS):
        padded = jnp.concatenate([object_field, jnp.zeros((2, PATCH, COLUMNS), object_field.dtype)], axis=1)

        def visit(carry, slot):
            grand, probe_sum = carry
            block_index = slot // SLOTS
            row = block_index * BLOCK_ROWS + offsets[slot, 0]
            column = offsets[slot, 1]
            anchor = (jnp.int32(0), row, column)
            patch_field = lax.dynamic_slice(padded, anchor, (2, PATCH, PATCH))
            far_real, far_imag, power = detector_waves(patch_field, probe_modes, cosine, sine_table)
            patch_grad, probe_grad = gradients(patch_field, probe_modes, far_real, far_imag, power, amplitudes[slot], cosine, sine_table)
            weight = (slot % SLOTS < counts[block_index]).astype(object_field.dtype)
            current = lax.dynamic_slice(grand, anchor, (2, PATCH, PATCH))
            grand = lax.dynamic_update_slice(grand, current + weight * patch_grad, anchor)
            return ((grand, probe_sum + weight * probe_grad), None)
        start = (jnp.zeros_like(padded), jnp.zeros_like(probe_modes))
        (grand, probe_sum), unused = lax.scan(visit, start, jnp.arange(N_DIFF * SLOTS, dtype=jnp.int32))
        smooth = object_field + OBJECT_STEP * grand[:, :total_rows]
        row_ids = jnp.arange(-1, total_rows + 1, dtype=jnp.int32)
        for sweep in range(PASSES):
            smooth = diffuse(jnp.pad(smooth, ((0, 0), (1, 1), (0, 0))), row_ids, total_rows)
        object_field = smooth
        probe_modes = probe_modes + probe_sum / N_DIFF
    return (object_field, probe_modes)
```

```python
import functools

import jax
import jax.numpy as jnp
import numpy as np
from jax import lax
from jax.experimental import pallas as pl
from jax.experimental.pallas import tpu as pltpu
from jax.sharding import Mesh
from jax.sharding import PartitionSpec as P


PASSES = 3
EDGE_SCALE = 1.0
DIFFUSION_RATE = 0.2
OBJECT_STEP = 0.25
HALO = 8
INTERPRET = False
F32 = jnp.float32
BF16 = jnp.bfloat16
DIFF = ("chip", "core")
VMEM = pl.BlockSpec(memory_space=pltpu.VMEM)
SMEM = pl.BlockSpec(memory_space=pltpu.SMEM)


def call(kernel, out_shape, in_specs, scratch=(), mib=8):
    single = not isinstance(out_shape, (tuple, list))
    return pl.pallas_call(
        kernel,
        out_shape=out_shape,
        in_specs=in_specs,
        out_specs=VMEM if single else [VMEM] * len(out_shape),
        scratch_shapes=list(scratch),
        compiler_params=pltpu.CompilerParams(vmem_limit_bytes=mib << 20),
        interpret=INTERPRET,
    )


def shape(*dims):
    return jax.ShapeDtypeStruct(dims, F32)


def tables(length):
    half = length // 2
    k = np.arange(half)[:, None]
    j = np.arange(half)[None, :]
    out = []
    for order in (2 * j, 2 * j + 1):
        angle = (k * order % length).astype(np.float64) * (2.0 * np.pi / length)
        c, s = np.cos(angle) / np.sqrt(length), np.sin(angle) / np.sqrt(length)
        block = np.block([[c, -s], [s, c]]).astype(np.float32)
        for table in (block, block.T):
            high = table.astype(BF16)
            out += [high, (table - high.astype(np.float32)).astype(BF16)]
    return np.stack(out)


def parity_order(length):
    half = length // 2
    order = np.zeros((length, length), np.float32)
    for q in range(2):
        order[2 * np.arange(half) + q, q * half + np.arange(half)] = 1.0
    return np.stack([order, order.T]).astype(BF16)


def halves(value):
    high = value.astype(BF16)
    low = (value - high.astype(F32)).astype(BF16)
    return high, low


def from_left(tab, which, value):
    high, low = halves(value)
    return jnp.dot(
        jnp.concatenate([tab[which], tab[which], tab[which + 1]], axis=1),
        jnp.concatenate([high, low, high], axis=0),
        preferred_element_type=F32,
    )


def from_right(value, tab, which):
    high, low = halves(value)
    return jnp.dot(
        jnp.concatenate([high, low, high], axis=1),
        jnp.concatenate([tab[which], tab[which], tab[which + 1]], axis=0),
        preferred_element_type=F32,
    )


def to_detector(tab, real, imag):
    h = real.shape[0] // 2
    cols = []
    for q in range(2):
        join = jnp.add if q == 0 else jnp.subtract
        pair = [join(v[:, :h], v[:, h:]) for v in (real, imag)]
        cols.append(from_right(jnp.concatenate(pair, axis=1), tab, 4 * q))
    out = []
    for p in range(2):
        join = jnp.add if p == 0 else jnp.subtract
        even, odd = [join(v[:h], v[h:]) for v in cols]
        data = jnp.concatenate(
            [
                jnp.concatenate([even[:, :h], odd[:, :h]], axis=1),
                jnp.concatenate([even[:, h:], odd[:, h:]], axis=1),
            ],
            axis=0,
        )
        out.append(from_left(tab, 4 * p + 2, data))
    return out


def to_sample(tab, even, odd):
    h = even.shape[0] // 2
    a = from_left(tab, 0, even)
    b = from_left(tab, 4, odd)
    top, low = a + b, a - b
    cols = []
    for q in range(2):
        lanes = slice(q * h, (q + 1) * h)
        data = jnp.concatenate(
            [
                jnp.concatenate([top[:h, lanes], low[:h, lanes]], axis=0),
                jnp.concatenate([top[h:, lanes], low[h:, lanes]], axis=0),
            ],
            axis=1,
        )
        cols.append(from_right(data, tab, 4 * q + 2))
    a, b = cols
    real = jnp.concatenate([a[:, :h] + b[:, :h], a[:, :h] - b[:, :h]], axis=1)
    imag = jnp.concatenate([a[:, h:] + b[:, h:], a[:, h:] - b[:, h:]], axis=1)
    return real, imag


def thirds(value):
    high = value.astype(BF16)
    left = value - high.astype(F32)
    mid = left.astype(BF16)
    return high, mid, (left - mid.astype(F32)).astype(BF16)


def amplitude_kernel(amp, order, out):
    slots, size = amp.shape[:2]
    half = size // 2
    for slot in range(slots):
        value = jnp.dot(
            jnp.concatenate(thirds(amp[slot] * 2.0**-8), axis=1),
            jnp.concatenate([order[0]] * 3, axis=0),
            preferred_element_type=F32,
        )
        value = jnp.dot(
            jnp.concatenate([order[1]] * 3, axis=1),
            jnp.concatenate(thirds(value), axis=0),
            preferred_element_type=F32,
        )
        for p in range(2):
            out[slot, p] = value[p * half : (p + 1) * half] * 2.0**8


def cut_kernel(offs, own, following, *pieces):
    half = own.shape[1]
    size = pieces[0].shape[2]
    row = lax.axis_index("obj") * half + lax.broadcasted_iota(jnp.int32, (half, size), 0)
    column = lax.broadcasted_iota(jnp.int32, (half, size), 1)
    for slot, piece in enumerate(pieces):
        here = row >= offs[slot, 0]
        inside = column >= offs[slot, 1]
        for part in range(2):
            near = jnp.where(here, own[part, :, :size], following[part, :, :size])
            far = jnp.where(here, own[part, :, size:], following[part, :, size:])
            piece[part] = jnp.where(inside, near, far)


def shifts(offs, slot, size, half):
    row = lax.rem(offs[slot, 0] - half * lax.axis_index("obj") + size, size)
    return row, lax.rem(offs[slot, 1], size)


def turned(value, rows, columns):
    return pltpu.roll(pltpu.roll(value, rows, 0), columns, 1)


def own_diff():
    return lax.axis_index("chip") * lax.axis_size("core") + lax.axis_index("core")


def slot_kernel(slot, last, offs, counts, mine, theirs, own, other_a, other_b, amp, tab, *rest):
    if last:
        before, grad_keep, grad_send, patch_grad, rest_far, field, far, grads, power = rest
    else:
        grads, patch_grad, rest_far, field, far, _, power = rest
    size = own.shape[-1]
    half = size // 2
    down, across = shifts(offs, slot, size, mine.shape[1])
    weight = (slot < counts[own_diff()]).astype(F32)
    for part in range(2):
        whole = jnp.concatenate([mine[part], theirs[part]], axis=0)
        field[part] = turned(whole, lax.rem(size - down, size), lax.rem(size - across, size))
    modes = (own.at[0], own.at[1], other_a, other_b)

    for mode in range(4):
        pr, pi = modes[mode][0], modes[mode][1]
        fr, fi = field[0], field[1]
        waves = to_detector(tab, pr * fr - pi * fi, pr * fi + pi * fr)
        for p in range(2):
            far[mode, p] = waves[p]
            amount = waves[p][:half] * waves[p][:half] + waves[p][half:] * waves[p][half:]
            power[p] = amount if mode == 0 else power[p] + amount
    for p in range(2):
        power[p] = amp[slot, p] / jnp.sqrt(power[p] + 1.0) - 1.0
    for mode in range(2):
        for p in range(2):
            for part in range(2):
                rows = slice(part * half, (part + 1) * half)
                rest_far[mode, p, rows] = far[2 + mode, p, rows] * power[p]

    for mode in range(2):
        scaled = [
            far[mode, p] * jnp.concatenate([power[p], power[p]], axis=0) for p in range(2)
        ]
        real, imag = to_sample(tab, *scaled)
        pr, pi = modes[mode][0], modes[mode][1]
        fr, fi = field[0], field[1]
        if mode == 0:
            patch_grad[0] = pr * real + pi * imag
            patch_grad[1] = pr * imag - pi * real
        else:
            patch_grad[0] += pr * real + pi * imag
            patch_grad[1] += pr * imag - pi * real
        grads[mode, 0] = weight * (fr * real + fi * imag)
        grads[mode, 1] = weight * (fr * imag - fi * real)
    if last:
        core = lax.axis_index("core")
        grad_keep[...] = before[core] + grads[core]
        grad_send[...] = before[1 - core] + grads[1 - core]


def spread_kernel(offs, counts, other_a, other_b, tab, grad_0, far_0, grad_1, far_1, own, spill, total):
    half = own.shape[1]
    size = total.shape[-1]
    row = lax.axis_index("obj") * half + lax.broadcasted_iota(jnp.int32, (half, size), 0)
    column = lax.broadcasted_iota(jnp.int32, (half, size), 1)
    for slot, (grad, far) in enumerate(((grad_0, far_0), (grad_1, far_1))):
        total[...] = grad[...]
        for mode, other in enumerate((other_a, other_b)):
            real, imag = to_sample(tab, far[mode, 0], far[mode, 1])
            pr, pi = other[0], other[1]
            total[0] += pr * real + pi * imag
            total[1] += pr * imag - pi * real
        down, across = shifts(offs, slot, size, half)
        here = row >= offs[slot, 0]
        inside = column >= offs[slot, 1]
        weight = (slot < counts[own_diff()]).astype(F32)
        for part in range(2):
            value = weight * turned(total[part], down, across)[:half]
            stay = jnp.where(here, value, 0.0)
            leave = value - stay
            for target, amount in ((own, stay), (spill, leave)):
                near = jnp.where(inside, amount, 0.0)
                if slot == 0:
                    target[part, :, :size] = near
                    target[part, :, size:] = amount - near
                else:
                    target[part, :, :size] += near
                    target[part, :, size:] += amount - near


def diffuse_kernel(total_rows, above, tile, below, out):
    rows = tile.shape[1]
    columns = tile.shape[2]
    flat = own_diff() * lax.axis_size("obj") + lax.axis_index("obj")
    full = rows + 2 * HALO
    row = flat * rows - HALO + lax.broadcasted_iota(jnp.int32, (full, columns), 0)
    column = lax.broadcasted_iota(jnp.int32, (full, columns), 1)
    has_below = (row >= 0) & (row < total_rows - 1)
    has_right = column < columns - 1
    now = [jnp.concatenate([above[p], tile[p], below[p]], axis=0) for p in range(2)]

    def flux(axis, length, valid):
        step = [pltpu.roll(v, length - 1, axis) - v for v in now]
        weight = 1.0 / (1.0 + (step[0] * step[0] + step[1] * step[1]) / (EDGE_SCALE * EDGE_SCALE))
        weight = jnp.where(valid, weight, 0.0)
        step = [s * weight for s in step]
        return [s - pltpu.roll(s, 1, axis) for s in step]

    for _ in range(PASSES):
        vertical = flux(0, full, has_below)
        sideways = flux(1, columns, has_right)
        now = [u + DIFFUSION_RATE * (v + s) for u, v, s in zip(now, vertical, sideways)]
    for p in range(2):
        out[p] = now[p][HALO : HALO + rows]


def shifted(value, axes, count, steps):
    return lax.ppermute(
        value, axes, [(i, i + steps) for i in range(count) if 0 <= i + steps < count]
    )


def body(object_field, probe_modes, amplitudes, offsets, counts):
    tile_rows, columns = object_field.shape[1:]
    size = probe_modes.shape[-1]
    n_chip, n_core, n_obj = (lax.axis_size(a) for a in ("chip", "core", "obj"))
    n_diff = n_chip * n_core
    total_rows = tile_rows * n_obj * n_diff
    core = lax.axis_index("core")
    swap = [(0, 1), (1, 0)]
    tab = jnp.asarray(tables(size))

    following = shifted(object_field, DIFF, n_diff, -1)
    mode = lax.dynamic_index_in_dim(probe_modes, core, 0, keepdims=False)
    other_a = lax.ppermute(mode, DIFF + ("obj",), probe_pairs(n_chip, n_obj))
    other_b = lax.ppermute(other_a, "core", swap)
    amp = call(
        amplitude_kernel, shape(amplitudes.shape[0], 2, size // 2, size), [VMEM, VMEM]
    )(amplitudes, jnp.asarray(parity_order(size)))
    piece = shape(2, tile_rows, size)
    mine = call(cut_kernel, [piece, piece], [SMEM, VMEM, VMEM])(offsets, object_field, following)
    theirs_0 = lax.ppermute(mine[0], "obj", swap)
    theirs_1 = lax.ppermute(mine[1], "obj", swap)

    both = shape(2, 2, size, size)
    patch = shape(2, size, size)
    scratch = [
        pltpu.VMEM((2, size, size), F32),
        pltpu.VMEM((4, 2, size, size), F32),
        pltpu.VMEM((2, 2, size, size), F32),
        pltpu.VMEM((2, size // 2, size), F32),
    ]
    specs = [SMEM, SMEM] + [VMEM] * 7
    grads, patch_0, far_0 = call(
        functools.partial(slot_kernel, 0, False),
        [both, patch, both], specs, scratch, 24,
    )(offsets, counts, mine[0], theirs_0, probe_modes, other_a, other_b, amp, tab)
    keep, send, patch_1, far_1 = call(
        functools.partial(slot_kernel, 1, True),
        [patch, patch, patch, both], specs + [VMEM], scratch, 24,
    )(offsets, counts, mine[1], theirs_1, probe_modes, other_a, other_b, amp, tab, grads)

    summed = keep + lax.ppermute(send, "core", swap)
    pieces = summed.reshape(n_chip, 2 * size // n_chip, size)
    gathered = lax.all_to_all(pieces, "chip", 0, 0)
    share = jnp.sum(gathered, axis=0)
    views = probe_modes.reshape(2, n_chip, 2 * size // n_chip, size)
    start = lax.dynamic_slice(
        views, (core, lax.axis_index("chip"), 0, 0), (1, 1) + views.shape[2:]
    )[0, 0]
    share = start + share / n_diff
    updated = lax.all_to_all(jnp.broadcast_to(share[None], pieces.shape), "chip", 0, 0)
    updated = updated.reshape(2, size, size)
    remote = lax.ppermute(updated, "core", swap)
    probe_out = jnp.where(
        core == 0, jnp.stack([updated, remote]), jnp.stack([remote, updated])
    )

    tile = shape(2, tile_rows, columns)
    own, spill = call(
        spread_kernel,
        [tile, tile],
        [SMEM, SMEM] + [VMEM] * 7,
        [pltpu.VMEM((2, size, size), F32)],
        16,
    )(offsets, counts, other_a, other_b, tab, patch_0, far_0, patch_1, far_1)
    arrived = shifted(spill, DIFF, n_diff, 1)
    raised = object_field + OBJECT_STEP * (own + arrived)
    flat = DIFF + ("obj",)
    above = shifted(raised[:, tile_rows - HALO :], flat, n_diff * n_obj, 1)
    below = shifted(raised[:, :HALO], flat, n_diff * n_obj, -1)
    smooth = call(
        functools.partial(diffuse_kernel, total_rows), tile, [VMEM] * 3, ()
    )(above, raised, below)
    return smooth, probe_out


def probe_pairs(n_chip, n_obj):
    def place(chip, core, obj):
        return (chip * 2 + core) * n_obj + obj

    return [
        (place(chip, core, obj), place(chip ^ core, core, 1 - obj))
        for chip in range(n_chip)
        for core in range(2)
        for obj in range(n_obj)
    ]


def solution(mesh):
    n_diff, n_obj = mesh.devices.shape
    fine = Mesh(mesh.devices.reshape(n_diff // 2, 2, n_obj), ("chip", "core", "obj"))
    placed = (
        P(None, ("chip", "core", "obj"), None),
        P("obj", None, None, None),
        P(DIFF, None, None),
        P(DIFF, None),
        P(),
    )
    return jax.shard_map(
        body,
        mesh=fine,
        in_specs=placed,
        out_specs=(P(None, ("chip", "core", "obj"), None), P("obj", None, None, None)),
        check_vma=False,
    )
```

```python
import functools

import jax
import jax.numpy as jnp
import numpy as np
from jax import lax
from jax.experimental import pallas as pl
from jax.experimental.pallas import tpu as pltpu
from jax.sharding import Mesh
from jax.sharding import PartitionSpec as P


PASSES = 3
EDGE_SCALE = 1.0
DIFFUSION_RATE = 0.2
OBJECT_STEP = 0.25
HALO = 8
INTERPRET = False
F32 = jnp.float32
BF16 = jnp.bfloat16
DIFF = ("chip", "core")
VMEM = pl.BlockSpec(memory_space=pltpu.VMEM)
SMEM = pl.BlockSpec(memory_space=pltpu.SMEM)


def call(kernel, out_shape, in_specs, scratch=(), mib=8):
    single = not isinstance(out_shape, (tuple, list))
    return pl.pallas_call(
        kernel,
        out_shape=out_shape,
        in_specs=in_specs,
        out_specs=VMEM if single else [VMEM] * len(out_shape),
        scratch_shapes=list(scratch),
        compiler_params=pltpu.CompilerParams(vmem_limit_bytes=mib << 20),
        interpret=INTERPRET,
    )


def shape(*dims):
    return jax.ShapeDtypeStruct(dims, F32)


def tables(length):
    half = length // 2
    k = np.arange(half)[:, None]
    j = np.arange(half)[None, :]
    out = []
    for order in (2 * j, 2 * j + 1):
        angle = (k * order % length).astype(np.float64) * (2.0 * np.pi / length)
        c, s = np.cos(angle) / np.sqrt(length), np.sin(angle) / np.sqrt(length)
        block = np.block([[c, -s], [s, c]]).astype(np.float32)
        for table in (block, block.T):
            high = table.astype(BF16)
            out += [high, (table - high.astype(np.float32)).astype(BF16)]
    return np.stack(out)


def parity_order(length):
    half = length // 2
    order = np.zeros((length, length), np.float32)
    for q in range(2):
        order[2 * np.arange(half) + q, q * half + np.arange(half)] = 1.0
    return np.stack([order, order.T]).astype(BF16)


def halves(value):
    high = value.astype(BF16)
    low = (value - high.astype(F32)).astype(BF16)
    return high, low


def from_left(tab, which, value):
    high, low = halves(value)
    return jnp.dot(
        jnp.concatenate([tab[which], tab[which], tab[which + 1]], axis=1),
        jnp.concatenate([high, low, high], axis=0),
        preferred_element_type=F32,
    )


def from_right(value, tab, which):
    high, low = halves(value)
    return jnp.dot(
        jnp.concatenate([high, low, high], axis=1),
        jnp.concatenate([tab[which], tab[which], tab[which + 1]], axis=0),
        preferred_element_type=F32,
    )


def to_detector(tab, real, imag):
    h = real.shape[0] // 2
    cols = []
    for q in range(2):
        join = jnp.add if q == 0 else jnp.subtract
        pair = [join(v[:, :h], v[:, h:]) for v in (real, imag)]
        cols.append(from_right(jnp.concatenate(pair, axis=1), tab, 4 * q))
    out = []
    for p in range(2):
        join = jnp.add if p == 0 else jnp.subtract
        even, odd = [join(v[:h], v[h:]) for v in cols]
        data = jnp.concatenate(
            [
                jnp.concatenate([even[:, :h], odd[:, :h]], axis=1),
                jnp.concatenate([even[:, h:], odd[:, h:]], axis=1),
            ],
            axis=0,
        )
        out.append(from_left(tab, 4 * p + 2, data))
    return out


def to_sample(tab, even, odd):
    h = even.shape[0] // 2
    a = from_left(tab, 0, even)
    b = from_left(tab, 4, odd)
    top, low = a + b, a - b
    cols = []
    for q in range(2):
        lanes = slice(q * h, (q + 1) * h)
        data = jnp.concatenate(
            [
                jnp.concatenate([top[:h, lanes], low[:h, lanes]], axis=0),
                jnp.concatenate([top[h:, lanes], low[h:, lanes]], axis=0),
            ],
            axis=1,
        )
        cols.append(from_right(data, tab, 4 * q + 2))
    a, b = cols
    real = jnp.concatenate([a[:, :h] + b[:, :h], a[:, :h] - b[:, :h]], axis=1)
    imag = jnp.concatenate([a[:, h:] + b[:, h:], a[:, h:] - b[:, h:]], axis=1)
    return real, imag


def thirds(value):
    high = value.astype(BF16)
    left = value - high.astype(F32)
    mid = left.astype(BF16)
    return high, mid, (left - mid.astype(F32)).astype(BF16)


def amplitude_kernel(amp, order, out):
    slots, size = amp.shape[:2]
    half = size // 2
    for slot in range(slots):
        value = jnp.dot(
            jnp.concatenate(thirds(amp[slot] * 2.0**-8), axis=1),
            jnp.concatenate([order[0]] * 3, axis=0),
            preferred_element_type=F32,
        )
        value = jnp.dot(
            jnp.concatenate([order[1]] * 3, axis=1),
            jnp.concatenate(thirds(value), axis=0),
            preferred_element_type=F32,
        )
        for p in range(2):
            out[slot, p] = value[p * half : (p + 1) * half] * 2.0**8


def cut_kernel(offs, own, following, *pieces):
    half = own.shape[1]
    size = pieces[0].shape[2]
    row = lax.axis_index("obj") * half + lax.broadcasted_iota(jnp.int32, (half, size), 0)
    column = lax.broadcasted_iota(jnp.int32, (half, size), 1)
    for slot, piece in enumerate(pieces):
        here = row >= offs[slot, 0]
        inside = column >= offs[slot, 1]
        for part in range(2):
            near = jnp.where(here, own[part, :, :size], following[part, :, :size])
            far = jnp.where(here, own[part, :, size:], following[part, :, size:])
            piece[part] = jnp.where(inside, near, far)


def shifts(offs, slot, size, half):
    row = lax.rem(offs[slot, 0] - half * lax.axis_index("obj") + size, size)
    return row, lax.rem(offs[slot, 1], size)


def turned(value, rows, columns):
    return pltpu.roll(pltpu.roll(value, rows, 0), columns, 1)


def own_diff():
    return lax.axis_index("chip") * lax.axis_size("core") + lax.axis_index("core")


def slot_kernel(slot, last, offs, counts, mine, theirs, own, other_a, other_b, amp, tab, *rest):
    if last:
        before, grad_keep, grad_send, extra, field, far, grads, power = rest
    else:
        grads, extra, field, far, _, power = rest
    size = own.shape[-1]
    half = size // 2
    down, across = shifts(offs, slot, size, mine.shape[1])
    weight = (slot < counts[own_diff()]).astype(F32)
    for part in range(2):
        whole = jnp.concatenate([mine[part], theirs[part]], axis=0)
        field[part] = turned(whole, lax.rem(size - down, size), lax.rem(size - across, size))
    modes = (own.at[0], own.at[1], other_a, other_b)

    for mode in range(4):
        pr, pi = modes[mode][0], modes[mode][1]
        fr, fi = field[0], field[1]
        waves = to_detector(tab, pr * fr - pi * fi, pr * fi + pi * fr)
        for p in range(2):
            far[mode, p] = waves[p]
            amount = waves[p][:half] * waves[p][:half] + waves[p][half:] * waves[p][half:]
            power[p] = amount if mode == 0 else power[p] + amount
    for p in range(2):
        power[p] = amp[slot, p] / jnp.sqrt(power[p] + 1.0) - 1.0
    for mode in range(2):
        for p in range(2):
            for part in range(2):
                rows = slice(part * half, (part + 1) * half)
                extra[mode, p, rows] = far[2 + mode, p, rows] * power[p]

    for mode in range(2):
        scaled = [
            far[mode, p] * jnp.concatenate([power[p], power[p]], axis=0) for p in range(2)
        ]
        real, imag = to_sample(tab, *scaled)
        pr, pi = modes[mode][0], modes[mode][1]
        fr, fi = field[0], field[1]
        if mode == 0:
            extra[2, 0] = pr * real + pi * imag
            extra[2, 1] = pr * imag - pi * real
        else:
            extra[2, 0] += pr * real + pi * imag
            extra[2, 1] += pr * imag - pi * real
        grads[mode, 0] = weight * (fr * real + fi * imag)
        grads[mode, 1] = weight * (fr * imag - fi * real)
    if last:
        core = lax.axis_index("core")
        grad_keep[...] = before[core] + grads[core]
        grad_send[...] = before[1 - core] + grads[1 - core]


def spread_kernel(offs, counts, other_a, other_b, tab, extra_0, extra_1, own, spill, total):
    half = own.shape[1]
    size = total.shape[-1]
    row = lax.axis_index("obj") * half + lax.broadcasted_iota(jnp.int32, (half, size), 0)
    column = lax.broadcasted_iota(jnp.int32, (half, size), 1)
    for slot, extra in enumerate((extra_0, extra_1)):
        total[...] = extra[2]
        for mode, other in enumerate((other_a, other_b)):
            real, imag = to_sample(tab, extra[mode, 0], extra[mode, 1])
            pr, pi = other[0], other[1]
            total[0] += pr * real + pi * imag
            total[1] += pr * imag - pi * real
        down, across = shifts(offs, slot, size, half)
        here = row >= offs[slot, 0]
        inside = column >= offs[slot, 1]
        weight = (slot < counts[own_diff()]).astype(F32)
        for part in range(2):
            value = weight * turned(total[part], down, across)[:half]
            stay = jnp.where(here, value, 0.0)
            leave = value - stay
            for target, amount in ((own, stay), (spill, leave)):
                near = jnp.where(inside, amount, 0.0)
                if slot == 0:
                    target[part, :, :size] = near
                    target[part, :, size:] = amount - near
                else:
                    target[part, :, :size] += near
                    target[part, :, size:] += amount - near


def diffuse_kernel(total_rows, outer, tile, inner, out):
    rows = tile.shape[1]
    columns = tile.shape[2]
    flat = own_diff() * lax.axis_size("obj") + lax.axis_index("obj")
    full = rows + 2 * HALO
    row = flat * rows - HALO + lax.broadcasted_iota(jnp.int32, (full, columns), 0)
    column = lax.broadcasted_iota(jnp.int32, (full, columns), 1)
    has_below = (row >= 0) & (row < total_rows - 1)
    has_right = column < columns - 1
    first = lax.axis_index("obj") == 0
    now = []
    for p in range(2):
        above = jnp.where(first, outer[p], inner[p])
        below = jnp.where(first, inner[p], outer[p])
        now.append(jnp.concatenate([above, tile[p], below], axis=0))

    def flux(axis, length, valid):
        step = [pltpu.roll(v, length - 1, axis) - v for v in now]
        weight = 1.0 / (1.0 + (step[0] * step[0] + step[1] * step[1]) / (EDGE_SCALE * EDGE_SCALE))
        weight = jnp.where(valid, weight, 0.0)
        step = [s * weight for s in step]
        return [s - pltpu.roll(s, 1, axis) for s in step]

    for _ in range(PASSES):
        vertical = flux(0, full, has_below)
        sideways = flux(1, columns, has_right)
        now = [u + DIFFUSION_RATE * (v + s) for u, v, s in zip(now, vertical, sideways)]
    for p in range(2):
        out[p] = now[p][HALO : HALO + rows]


def shifted(value, axes, count, steps):
    return lax.ppermute(
        value, axes, [(i, i + steps) for i in range(count) if 0 <= i + steps < count]
    )


def body(object_field, probe_modes, amplitudes, offsets, counts):
    tile_rows, columns = object_field.shape[1:]
    size = probe_modes.shape[-1]
    n_chip, n_core, n_obj = (lax.axis_size(a) for a in ("chip", "core", "obj"))
    n_diff = n_chip * n_core
    total_rows = tile_rows * n_obj * n_diff
    core = lax.axis_index("core")
    swap = [(0, 1), (1, 0)]
    tab = jnp.asarray(tables(size))

    following = shifted(object_field, DIFF, n_diff, -1)
    mode = lax.dynamic_index_in_dim(probe_modes, core, 0, keepdims=False)
    other_a = lax.ppermute(mode, DIFF + ("obj",), probe_pairs(n_chip, n_obj))
    other_b = lax.ppermute(other_a, "core", swap)
    amp = call(
        amplitude_kernel, shape(amplitudes.shape[0], 2, size // 2, size), [VMEM, VMEM]
    )(amplitudes, jnp.asarray(parity_order(size)))
    piece = shape(2, tile_rows, size)
    mine = call(cut_kernel, [piece, piece], [SMEM, VMEM, VMEM])(offsets, object_field, following)
    theirs_0 = lax.ppermute(mine[0], "obj", swap)
    theirs_1 = lax.ppermute(mine[1], "obj", swap)

    both = shape(2, 2, size, size)
    patch = shape(2, size, size)
    more = shape(3, 2, size, size)
    scratch = [
        pltpu.VMEM((2, size, size), F32),
        pltpu.VMEM((4, 2, size, size), F32),
        pltpu.VMEM((2, 2, size, size), F32),
        pltpu.VMEM((2, size // 2, size), F32),
    ]
    specs = [SMEM, SMEM] + [VMEM] * 7
    grads, extra_0 = call(
        functools.partial(slot_kernel, 0, False),
        [both, more], specs, scratch, 24,
    )(offsets, counts, mine[0], theirs_0, probe_modes, other_a, other_b, amp, tab)
    keep, send, extra_1 = call(
        functools.partial(slot_kernel, 1, True),
        [patch, patch, more], specs + [VMEM], scratch, 24,
    )(offsets, counts, mine[1], theirs_1, probe_modes, other_a, other_b, amp, tab, grads)

    summed = keep + lax.ppermute(send, "core", swap)
    pieces = summed.reshape(n_chip, 2 * size // n_chip, size)
    gathered = lax.all_to_all(pieces, "chip", 0, 0)
    share = jnp.sum(gathered, axis=0)
    views = probe_modes.reshape(2, n_chip, 2 * size // n_chip, size)
    start = lax.dynamic_slice(
        views, (core, lax.axis_index("chip"), 0, 0), (1, 1) + views.shape[2:]
    )[0, 0]
    share = start + share / n_diff
    updated = lax.all_to_all(jnp.broadcast_to(share[None], pieces.shape), "chip", 0, 0)
    updated = updated.reshape(2, size, size)
    remote = lax.ppermute(updated, "core", swap)
    probe_out = jnp.where(
        core == 0, jnp.stack([updated, remote]), jnp.stack([remote, updated])
    )

    tile = shape(2, tile_rows, columns)
    own, spill = call(
        spread_kernel,
        [tile, tile],
        [SMEM, SMEM] + [VMEM] * 5,
        [pltpu.VMEM((2, size, size), F32)],
        16,
    )(offsets, counts, other_a, other_b, tab, extra_0, extra_1)
    arrived = shifted(spill, DIFF, n_diff, 1)
    raised = object_field + OBJECT_STEP * (own + arrived)
    flat = DIFF + ("obj",)
    first = lax.axis_index("obj") == 0
    top, low = raised[:, :HALO], raised[:, tile_rows - HALO :]
    count = n_diff * n_obj
    apart = [(i, j) for k in range(1, count - 1, 2) for i, j in ((k, k + 1), (k + 1, k))]
    outer = lax.ppermute(jnp.where(first, top, low), flat, apart)
    inner = lax.ppermute(jnp.where(first, low, top), "obj", swap)
    smooth = call(
        functools.partial(diffuse_kernel, total_rows), tile, [VMEM] * 3, ()
    )(outer, raised, inner)
    return smooth, probe_out


def probe_pairs(n_chip, n_obj):
    def place(chip, core, obj):
        return (chip * 2 + core) * n_obj + obj

    return [
        (place(chip, core, obj), place(chip ^ core, core, 1 - obj))
        for chip in range(n_chip)
        for core in range(2)
        for obj in range(n_obj)
    ]


def solution(mesh):
    n_diff, n_obj = mesh.devices.shape
    fine = Mesh(mesh.devices.reshape(n_diff // 2, 2, n_obj), ("chip", "core", "obj"))
    placed = (
        P(None, ("chip", "core", "obj"), None),
        P("obj", None, None, None),
        P(DIFF, None, None),
        P(DIFF, None),
        P(),
    )
    return jax.shard_map(
        body,
        mesh=fine,
        in_specs=placed,
        out_specs=(P(None, ("chip", "core", "obj"), None), P("obj", None, None, None)),
        check_vma=False,
    )
```

```python
import functools

import jax
import jax.numpy as jnp
import numpy as np
from jax import lax
from jax.experimental import pallas as pl
from jax.experimental.pallas import tpu as pltpu
from jax.sharding import Mesh
from jax.sharding import PartitionSpec as P


PASSES = 3
EDGE_SCALE = 1.0
DIFFUSION_RATE = 0.2
OBJECT_STEP = 0.25
HALO = 8
INTERPRET = False
F32 = jnp.float32
BF16 = jnp.bfloat16
DIFF = ("chip", "core")
VMEM = pl.BlockSpec(memory_space=pltpu.VMEM)
SMEM = pl.BlockSpec(memory_space=pltpu.SMEM)
HBM = pl.BlockSpec(memory_space=pltpu.HBM)


def call(kernel, out_shape, in_specs, scratch=(), mib=8, out_specs=None):
    single = not isinstance(out_shape, (tuple, list))
    if out_specs is None:
        out_specs = VMEM if single else [VMEM] * len(out_shape)
    return pl.pallas_call(
        kernel,
        out_shape=out_shape,
        in_specs=in_specs,
        out_specs=out_specs,
        scratch_shapes=list(scratch),
        compiler_params=pltpu.CompilerParams(vmem_limit_bytes=mib << 20),
        interpret=INTERPRET,
    )


def shape(*dims):
    return jax.ShapeDtypeStruct(dims, F32)


def tables(length):
    half = length // 2
    k = np.arange(half)[:, None]
    j = np.arange(half)[None, :]
    out = []
    for order in (2 * j, 2 * j + 1):
        angle = (k * order % length).astype(np.float64) * (2.0 * np.pi / length)
        c, s = np.cos(angle) / np.sqrt(length), np.sin(angle) / np.sqrt(length)
        block = np.block([[c, -s], [s, c]]).astype(np.float32)
        for table in (block, block.T):
            high = table.astype(BF16)
            out += [high, (table - high.astype(np.float32)).astype(BF16)]
    return np.stack(out)


def parity_order(length):
    half = length // 2
    order = np.zeros((length, length), np.float32)
    for q in range(2):
        order[2 * np.arange(half) + q, q * half + np.arange(half)] = 1.0
    return np.stack([order, order.T]).astype(BF16)


def halves(value):
    high = value.astype(BF16)
    low = (value - high.astype(F32)).astype(BF16)
    return high, low


def from_left(tab, which, value):
    high, low = halves(value)
    return jnp.dot(
        jnp.concatenate([tab[which], tab[which], tab[which + 1]], axis=1),
        jnp.concatenate([high, low, high], axis=0),
        preferred_element_type=F32,
    )


def from_right(value, tab, which):
    high, low = halves(value)
    return jnp.dot(
        jnp.concatenate([high, low, high], axis=1),
        jnp.concatenate([tab[which], tab[which], tab[which + 1]], axis=0),
        preferred_element_type=F32,
    )


def to_detector(tab, real, imag):
    h = real.shape[0] // 2
    cols = []
    for q in range(2):
        join = jnp.add if q == 0 else jnp.subtract
        pair = [join(v[:, :h], v[:, h:]) for v in (real, imag)]
        cols.append(from_right(jnp.concatenate(pair, axis=1), tab, 4 * q))
    out = []
    for p in range(2):
        join = jnp.add if p == 0 else jnp.subtract
        even, odd = [join(v[:h], v[h:]) for v in cols]
        data = jnp.concatenate(
            [
                jnp.concatenate([even[:, :h], odd[:, :h]], axis=1),
                jnp.concatenate([even[:, h:], odd[:, h:]], axis=1),
            ],
            axis=0,
        )
        out.append(from_left(tab, 4 * p + 2, data))
    return out


def to_sample(tab, even, odd):
    h = even.shape[0] // 2
    a = from_left(tab, 0, even)
    b = from_left(tab, 4, odd)
    top, low = a + b, a - b
    cols = []
    for q in range(2):
        lanes = slice(q * h, (q + 1) * h)
        data = jnp.concatenate(
            [
                jnp.concatenate([top[:h, lanes], low[:h, lanes]], axis=0),
                jnp.concatenate([top[h:, lanes], low[h:, lanes]], axis=0),
            ],
            axis=1,
        )
        cols.append(from_right(data, tab, 4 * q + 2))
    a, b = cols
    real = jnp.concatenate([a[:, :h] + b[:, :h], a[:, :h] - b[:, :h]], axis=1)
    imag = jnp.concatenate([a[:, h:] + b[:, h:], a[:, h:] - b[:, h:]], axis=1)
    return real, imag


def thirds(value):
    high = value.astype(BF16)
    left = value - high.astype(F32)
    mid = left.astype(BF16)
    return high, mid, (left - mid.astype(F32)).astype(BF16)


def amplitude_kernel(amp, order, out):
    slots, size = amp.shape[:2]
    half = size // 2
    for slot in range(slots):
        value = jnp.dot(
            jnp.concatenate(thirds(amp[slot] * 2.0**-8), axis=1),
            jnp.concatenate([order[0]] * 3, axis=0),
            preferred_element_type=F32,
        )
        value = jnp.dot(
            jnp.concatenate([order[1]] * 3, axis=1),
            jnp.concatenate(thirds(value), axis=0),
            preferred_element_type=F32,
        )
        for p in range(2):
            out[slot, p] = value[p * half : (p + 1) * half] * 2.0**8


def cut_kernel(offs, own, following, *pieces):
    half = own.shape[1]
    size = pieces[0].shape[2]
    row = lax.axis_index("obj") * half + lax.broadcasted_iota(jnp.int32, (half, size), 0)
    column = lax.broadcasted_iota(jnp.int32, (half, size), 1)
    for slot, piece in enumerate(pieces):
        here = row >= offs[slot, 0]
        inside = column >= offs[slot, 1]
        for part in range(2):
            near = jnp.where(here, own[part, :, :size], following[part, :, :size])
            far = jnp.where(here, own[part, :, size:], following[part, :, size:])
            piece[part] = jnp.where(inside, near, far)


def shifts(offs, slot, size, half):
    row = lax.rem(offs[slot, 0] - half * lax.axis_index("obj") + size, size)
    return row, lax.rem(offs[slot, 1], size)


def turned(value, rows, columns):
    return pltpu.roll(pltpu.roll(value, rows, 0), columns, 1)


def own_diff():
    return lax.axis_index("chip") * lax.axis_size("core") + lax.axis_index("core")


def slot_kernel(slot, last, offs, counts, mine, theirs, own, other_a, other_b, amp, tab, *rest):
    if last:
        before, grad_keep, grad_send, extra_out, field, far, grads, power, extra, sem = rest
    else:
        grads, extra, field, far, _, power = rest
    size = own.shape[-1]
    half = size // 2
    down, across = shifts(offs, slot, size, mine.shape[1])
    weight = (slot < counts[own_diff()]).astype(F32)
    for part in range(2):
        whole = jnp.concatenate([mine[part], theirs[part]], axis=0)
        field[part] = turned(whole, lax.rem(size - down, size), lax.rem(size - across, size))
    modes = (own.at[0], own.at[1], other_a, other_b)

    for mode in range(4):
        pr, pi = modes[mode][0], modes[mode][1]
        fr, fi = field[0], field[1]
        waves = to_detector(tab, pr * fr - pi * fi, pr * fi + pi * fr)
        for p in range(2):
            far[mode, p] = waves[p]
            amount = waves[p][:half] * waves[p][:half] + waves[p][half:] * waves[p][half:]
            power[p] = amount if mode == 0 else power[p] + amount
    for p in range(2):
        power[p] = amp[slot, p] / jnp.sqrt(power[p] + 1.0) - 1.0
    for mode in range(2):
        for p in range(2):
            for part in range(2):
                rows = slice(part * half, (part + 1) * half)
                extra[mode, p, rows] = far[2 + mode, p, rows] * power[p]

    for mode in range(2):
        scaled = [
            far[mode, p] * jnp.concatenate([power[p], power[p]], axis=0) for p in range(2)
        ]
        real, imag = to_sample(tab, *scaled)
        pr, pi = modes[mode][0], modes[mode][1]
        fr, fi = field[0], field[1]
        if mode == 0:
            extra[2, 0] = pr * real + pi * imag
            extra[2, 1] = pr * imag - pi * real
        else:
            extra[2, 0] += pr * real + pi * imag
            extra[2, 1] += pr * imag - pi * real
        grads[mode, 0] = weight * (fr * real + fi * imag)
        grads[mode, 1] = weight * (fr * imag - fi * real)
    if last:
        saved = pltpu.make_async_copy(extra, extra_out, sem)
        saved.start()
        core = lax.axis_index("core")
        grad_keep[...] = before[core] + grads[core]
        grad_send[...] = before[1 - core] + grads[1 - core]
        saved.wait()


def spread_kernel(offs, counts, other_a, other_b, tab, extra_0, extra_1, own, spill, total):
    half = own.shape[1]
    size = total.shape[-1]
    row = lax.axis_index("obj") * half + lax.broadcasted_iota(jnp.int32, (half, size), 0)
    column = lax.broadcasted_iota(jnp.int32, (half, size), 1)
    for slot, extra in enumerate((extra_0, extra_1)):
        total[...] = extra[2]
        for mode, other in enumerate((other_a, other_b)):
            real, imag = to_sample(tab, extra[mode, 0], extra[mode, 1])
            pr, pi = other[0], other[1]
            total[0] += pr * real + pi * imag
            total[1] += pr * imag - pi * real
        down, across = shifts(offs, slot, size, half)
        here = row >= offs[slot, 0]
        inside = column >= offs[slot, 1]
        weight = (slot < counts[own_diff()]).astype(F32)
        for part in range(2):
            value = weight * turned(total[part], down, across)[:half]
            stay = jnp.where(here, value, 0.0)
            leave = value - stay
            for target, amount in ((own, stay), (spill, leave)):
                near = jnp.where(inside, amount, 0.0)
                if slot == 0:
                    target[part, :, :size] = near
                    target[part, :, size:] = amount - near
                else:
                    target[part, :, :size] += near
                    target[part, :, size:] += amount - near


def share_kernel(n_diff, gathered, start, out):
    parts = [gathered[i] for i in range(8)]
    for chip in range(8, gathered.shape[0]):
        parts[chip % 8] += gathered[chip]
    while len(parts) > 1:
        parts = [a + b for a, b in zip(parts[::2], parts[1::2])]
    share = start[...] + parts[0] / n_diff
    for chip in range(gathered.shape[0]):
        out[chip] = share


def order_kernel(updated, remote, out, sems):
    core = lax.axis_index("core")
    mine = pltpu.make_async_copy(updated, out.at[core], sems.at[0])
    other = pltpu.make_async_copy(remote, out.at[1 - core], sems.at[1])
    mine.start()
    other.start()
    mine.wait()
    other.wait()


def diffuse_kernel(total_rows, outer, tile, inner, out):
    rows = tile.shape[1]
    columns = tile.shape[2]
    flat = own_diff() * lax.axis_size("obj") + lax.axis_index("obj")
    full = rows + 2 * HALO
    row = flat * rows - HALO + lax.broadcasted_iota(jnp.int32, (full, columns), 0)
    column = lax.broadcasted_iota(jnp.int32, (full, columns), 1)
    has_below = (row >= 0) & (row < total_rows - 1)
    has_right = column < columns - 1
    first = lax.axis_index("obj") == 0
    now = []
    for p in range(2):
        above = jnp.where(first, outer[p], inner[p])
        below = jnp.where(first, inner[p], outer[p])
        now.append(jnp.concatenate([above, tile[p], below], axis=0))

    def flux(axis, length, valid):
        step = [pltpu.roll(v, length - 1, axis) - v for v in now]
        weight = 1.0 / (1.0 + (step[0] * step[0] + step[1] * step[1]) / (EDGE_SCALE * EDGE_SCALE))
        weight = jnp.where(valid, weight, 0.0)
        step = [s * weight for s in step]
        return [s - pltpu.roll(s, 1, axis) for s in step]

    for _ in range(PASSES):
        vertical = flux(0, full, has_below)
        sideways = flux(1, columns, has_right)
        now = [u + DIFFUSION_RATE * (v + s) for u, v, s in zip(now, vertical, sideways)]
    for p in range(2):
        out[p] = now[p][HALO : HALO + rows]


def shifted(value, axes, count, steps):
    return lax.ppermute(
        value, axes, [(i, i + steps) for i in range(count) if 0 <= i + steps < count]
    )


def body(object_field, probe_modes, amplitudes, offsets, counts):
    tile_rows, columns = object_field.shape[1:]
    size = probe_modes.shape[-1]
    n_chip, n_core, n_obj = (lax.axis_size(a) for a in ("chip", "core", "obj"))
    n_diff = n_chip * n_core
    total_rows = tile_rows * n_obj * n_diff
    core = lax.axis_index("core")
    swap = [(0, 1), (1, 0)]
    tab = jnp.asarray(tables(size))

    following = shifted(object_field, DIFF, n_diff, -1)
    mode = lax.dynamic_index_in_dim(probe_modes, core, 0, keepdims=False)
    other_a = lax.ppermute(mode, DIFF + ("obj",), probe_pairs(n_chip, n_obj))
    other_b = lax.ppermute(other_a, "core", swap)
    amp = call(
        amplitude_kernel, shape(amplitudes.shape[0], 2, size // 2, size), [VMEM, VMEM]
    )(amplitudes, jnp.asarray(parity_order(size)))
    piece = shape(2, tile_rows, size)
    mine = call(cut_kernel, [piece, piece], [SMEM, VMEM, VMEM])(offsets, object_field, following)
    theirs_0 = lax.ppermute(mine[0], "obj", swap)
    theirs_1 = lax.ppermute(mine[1], "obj", swap)

    both = shape(2, 2, size, size)
    patch = shape(2, size, size)
    more = shape(3, 2, size, size)
    scratch = [
        pltpu.VMEM((2, size, size), F32),
        pltpu.VMEM((4, 2, size, size), F32),
        pltpu.VMEM((2, 2, size, size), F32),
        pltpu.VMEM((2, size // 2, size), F32),
    ]
    specs = [SMEM, SMEM] + [VMEM] * 7
    grads, extra_0 = call(
        functools.partial(slot_kernel, 0, False),
        [both, more], specs, scratch, 24,
    )(offsets, counts, mine[0], theirs_0, probe_modes, other_a, other_b, amp, tab)
    keep, send, extra_1 = call(
        functools.partial(slot_kernel, 1, True),
        [patch, patch, pltpu.HBM(more.shape, F32)], specs + [VMEM],
        scratch + [pltpu.VMEM(more.shape, F32), pltpu.SemaphoreType.DMA], 24,
        [VMEM, VMEM, HBM],
    )(offsets, counts, mine[1], theirs_1, probe_modes, other_a, other_b, amp, tab, grads)

    summed = keep + lax.ppermute(send, "core", swap)
    pieces = summed.reshape(n_chip, 2 * size // n_chip, size)
    gathered = lax.all_to_all(pieces, "chip", 0, 0)
    views = probe_modes.reshape(2, n_chip, 2 * size // n_chip, size)
    start = lax.dynamic_slice(
        views, (core, lax.axis_index("chip"), 0, 0), (1, 1) + views.shape[2:]
    )[0, 0]
    share = call(
        functools.partial(share_kernel, n_diff), shape(*pieces.shape), [VMEM] * 2
    )(gathered, start)
    updated = lax.all_to_all(share, "chip", 0, 0)
    updated = updated.reshape(2, size, size)
    remote = lax.ppermute(updated, "core", swap)
    probe_out = call(
        order_kernel,
        pltpu.HBM((2, 2, size, size), F32),
        [VMEM, VMEM],
        [pltpu.SemaphoreType.DMA((2,))],
        4,
        HBM,
    )(updated, remote)

    tile = shape(2, tile_rows, columns)
    own, spill = call(
        spread_kernel,
        [tile, tile],
        [SMEM, SMEM] + [VMEM] * 5,
        [pltpu.VMEM((2, size, size), F32)],
        16,
    )(offsets, counts, other_a, other_b, tab, extra_0, extra_1)
    arrived = shifted(spill, DIFF, n_diff, 1)
    raised = object_field + OBJECT_STEP * (own + arrived)
    flat = DIFF + ("obj",)
    first = lax.axis_index("obj") == 0
    top, low = raised[:, :HALO], raised[:, tile_rows - HALO :]
    count = n_diff * n_obj
    apart = [(i, j) for k in range(1, count - 1, 2) for i, j in ((k, k + 1), (k + 1, k))]
    outer = lax.ppermute(jnp.where(first, top, low), flat, apart)
    inner = lax.ppermute(jnp.where(first, low, top), "obj", swap)
    smooth = call(
        functools.partial(diffuse_kernel, total_rows), tile, [VMEM] * 3, ()
    )(outer, raised, inner)
    return smooth, probe_out


def probe_pairs(n_chip, n_obj):
    def place(chip, core, obj):
        return (chip * 2 + core) * n_obj + obj

    return [
        (place(chip, core, obj), place(chip ^ core, core, 1 - obj))
        for chip in range(n_chip)
        for core in range(2)
        for obj in range(n_obj)
    ]


def solution(mesh):
    n_diff, n_obj = mesh.devices.shape
    fine = Mesh(mesh.devices.reshape(n_diff // 2, 2, n_obj), ("chip", "core", "obj"))
    placed = (
        P(None, ("chip", "core", "obj"), None),
        P("obj", None, None, None),
        P(DIFF, None, None),
        P(DIFF, None),
        P(),
    )
    return jax.shard_map(
        body,
        mesh=fine,
        in_specs=placed,
        out_specs=(P(None, ("chip", "core", "obj"), None), P("obj", None, None, None)),
        check_vma=False,
    )
```
